32 devices in a mesh: band: 4 (over x, core), slab: 8 (over z, y).
Axes of the slice: x: 2, y: 2, z: 4, core: 2. Of those that a mesh axis runs over, the one named last changes fastest.
Arguments:
- orbitals: float32 [12, 128, 128, 128], P('band', 'slab'), may hold values from -6 to 6
- occupation: float32 [12], replicated, may hold values from 0.2 to 2
- assignment: int32 [12], P('band'), may hold values from 0 to 11, each once
- pair_live: int32 [12, 12], P('band'), may hold values from 0 to 1, as said below
Outputs:
- exchange: float32 [12, 128, 128, 128], P('band', 'slab')
The draws below stay inside these ranges and needn't reach their ends.
Inputs may be any that keep to these rules, and one draw needn't show every extreme that they name: `assignment`: every band number appears in exactly one slot. pair_live[s, t] equals pair_live[t, s].
All inputs are finite; a program needn't handle non-finite values.
Results may differ from the reference program's by a relative error of at most 0.00016.
Values sent between devices are 32-bit elements; how exact they have to be, the bound alone decides.
A program may use at most 64 MiB of HBM per device.

```python
import jax
import jax.numpy as jnp
from jax import lax

GRID = 128
ORB_GRP = 3
ORBITALS = 12
N_BAND = 4


def draw_pair_live(key, part):
    picks = jax.random.randint(key, (ORBITALS, ORBITALS), 0, 4)
    strict = jnp.triu(picks, 1)
    mirrored = strict + strict.T
    return jnp.minimum(mirrored, 1).astype(jnp.int32)


def steps_of(rng, dims, shards, smallest, high):
    level, own = 1.0, jax.random.fold_in(rng, 6)
    for dim, shards_of in shards:
        steps = jnp.exp(jax.random.uniform(jax.random.fold_in(own, dim), (shards_of,), jnp.float32, smallest / len(shards), high / len(shards)))
        level = level * jnp.repeat(steps, dims[dim] // shards_of).reshape([-1 if axis == dim else 1 for axis in range(len(dims))])
    return level


def centred(rng, shape, width, reach, split=(), kind=jnp.bfloat16):
    level = steps_of(rng, shape, split, -0.22, 0.18) if split else 1.0
    entries = jax.random.normal(rng, shape, jnp.float32) * width * level
    return jnp.minimum(jnp.maximum(entries, -reach), reach).astype(kind)


def setup_inputs(seed: int = 0) -> dict:
    seeds = jax.random.split(jax.random.key(seed), 5)
    orbitals = centred(seeds[0], (ORBITALS, GRID, GRID, GRID), 1.0, 6.0, ((0, 4), (1, 8)), jnp.float32)
    occupation = jnp.clip(jax.random.uniform(seeds[1], (ORBITALS,), jnp.float32, 0.2, 2.0), 0.2, 2.0)
    assignment = jax.random.permutation(seeds[2], ORBITALS).astype(jnp.int32)
    pair_live = draw_pair_live(jax.random.fold_in(seeds[4], 71), 0)
    return {"orbitals": orbitals, "occupation": occupation, "assignment": assignment, "pair_live": pair_live}


highest = lax.Precision.HIGHEST
screening = 0.01
lateral = 0.01

def sine_table(points):
    numbers = jnp.arange(points, dtype=jnp.float32) + 1.0
    return jnp.sqrt(2.0 / (points + 1.0)) * jnp.sin(jnp.pi * numbers[:, None] * numbers[None, :] / (points + 1.0))

def eigen_values(points):
    numbers = jnp.arange(points, dtype=jnp.float32) + 1.0
    return 2.0 - 2.0 * jnp.cos(jnp.pi * numbers / (points + 1.0))

def screened_solve(density):
    points = density.shape[-1]
    sine_rows = sine_table(points)
    spectra = jnp.einsum('pzyx,ax->pzya', density, sine_rows, precision=highest)
    spectra = jnp.einsum('pzya,by->pzba', spectra, sine_rows, precision=highest)
    spectra = jnp.einsum('pzba,cz->pcba', spectra, sine_rows, precision=highest)
    eigen_list = eigen_values(points)
    spectra = spectra / (eigen_list[:, None, None] + lateral * (eigen_list[None, :, None] + eigen_list[None, None, :]) + screening)
    spectra = jnp.einsum('pcba,cz->pzba', spectra, sine_rows, precision=highest)
    spectra = jnp.einsum('pzba,by->pzya', spectra, sine_rows, precision=highest)
    return jnp.einsum('pzya,ax->pzyx', spectra, sine_rows, precision=highest)

def reference(orbitals, occupation, assignment, pair_live):
    weights = occupation[assignment]
    live_pairs = pair_live.astype(jnp.float32)
    exchange_sum = jnp.zeros_like(orbitals)
    members = jnp.arange(ORB_GRP, dtype=jnp.int32)
    for block_index in range(N_BAND):
        neighbour = (block_index + 1) % N_BAND
        start_slot = neighbour * ORB_GRP
        visitors = orbitals[start_slot:start_slot + ORB_GRP]
        visit_weight = weights[start_slot:start_slot + ORB_GRP]

        def per_member(running, member):
            slot_index = block_index * ORB_GRP + member
            resident = lax.dynamic_index_in_dim(orbitals, slot_index, 0, keepdims=False)
            potential = screened_solve(resident[None] * visitors)
            live_row = lax.dynamic_index_in_dim(live_pairs, slot_index, 0, keepdims=False)[start_slot:start_slot + ORB_GRP]
            own_term = -lax.optimization_barrier(jnp.sum((live_row * visit_weight)[:, None, None, None] * potential * visitors, axis=0))
            resident_weight = lax.dynamic_index_in_dim(weights, slot_index, 0, keepdims=False)
            visit_term = -(live_row * resident_weight)[:, None, None, None] * potential * resident[None]
            running = running.at[slot_index].add(own_term)
            running = running.at[start_slot:start_slot + ORB_GRP].add(visit_term)
            return (running, None)
        exchange_sum, _ = lax.scan(per_member, exchange_sum, members)
    return exchange_sum
```

```python
import functools

import jax
import jax.numpy as jnp
import numpy as np
from jax import lax
from jax.experimental import pallas as pl
from jax.experimental.pallas import tpu as pltpu
from jax.sharding import PartitionSpec as P

screening = 0.01
lateral = 0.01
MESH = pl.DeviceIdType.MESH


def tables(points):
    numbers = np.arange(points, dtype=np.float64) + 1.0
    sine = np.sqrt(2.0 / (points + 1.0)) * np.sin(
        np.pi * numbers[:, None] * numbers[None, :] / (points + 1.0)
    )
    eigen = 2.0 - 2.0 * np.cos(np.pi * numbers / (points + 1.0))
    sine = sine.astype(np.float32)
    high = sine.astype(jnp.bfloat16)
    low = (sine - high.astype(np.float32)).astype(jnp.bfloat16)
    half = np.concatenate([high, low], axis=1)
    right = np.concatenate([half, half], axis=0)
    diagonal = 2.0 + lateral * (eigen[:, None] + eigen[None, :]) + screening
    return right, np.ascontiguousarray(right.T), diagonal.astype(np.float32)


def split(value):
    high = value.astype(jnp.bfloat16)
    low = (value - high.astype(jnp.float32)).astype(jnp.bfloat16)
    return high, low


def plane_pair(first, second, right, left):
    points = first.shape[0]
    high, low = split(jnp.concatenate([first, second], axis=0))
    both = jnp.dot(
        jnp.concatenate([high, low], axis=1), right, preferred_element_type=jnp.float32
    )
    rows = both[:, :points] + both[:, points:]
    high, low = split(rows)
    stacked = jnp.concatenate(
        [
            jnp.concatenate([high[:points], high[points:]], axis=1),
            jnp.concatenate([low[:points], low[points:]], axis=1),
        ],
        axis=0,
    )
    both = jnp.dot(left, stacked, preferred_element_type=jnp.float32)
    result = both[:points] + both[points:]
    return result[:, :points], result[:, points:]


def kernel(
    bands, slabs,
    orbitals, occupation, assignment, live, right_ref, left_ref, diagonal_ref,
    out,
    visitors, visit_sum, returned, spectra, down_in, down_out, up_in, up_out,
    pivots, reach, coefs, weight_out, weight_in,
    send_orb, recv_orb, send_weight, recv_weight, send_back, recv_back,
    send_down, recv_down, send_up, recv_up,
):
    members, planes, points, _ = orbitals.shape
    pairs = members * members
    band = lax.axis_index("band")
    slab = lax.axis_index("slab")
    above = lax.rem(band + 1, bands)
    below = lax.rem(band + bands - 1, bands)
    first, last = slab == 0, slab == slabs - 1

    barrier = pltpu.get_barrier_semaphore()
    for neighbour in (above, below):
        pl.semaphore_signal(barrier, inc=1, device_id=(neighbour, slab), device_id_type=MESH)

    @pl.when(jnp.logical_not(first))
    def _():
        pl.semaphore_signal(barrier, inc=1, device_id=(band, slab - 1), device_id_type=MESH)

    @pl.when(jnp.logical_not(last))
    def _():
        pl.semaphore_signal(barrier, inc=1, device_id=(band, slab + 1), device_id_type=MESH)

    weights = [occupation[assignment[k]] for k in range(members)]
    for k in range(members):
        weight_out[k] = jnp.full(weight_out.shape[1:], weights[k], jnp.float32)

    pl.semaphore_wait(barrier, 4 - first.astype(jnp.int32) - last.astype(jnp.int32))

    def remote(source, target, sent, landed, device):
        return pltpu.make_async_remote_copy(
            src_ref=source, dst_ref=target, send_sem=sent, recv_sem=landed,
            device_id=device, device_id_type=MESH,
        )

    def orb_copy(k):
        return remote(orbitals.at[k], visitors.at[k], send_orb.at[k], recv_orb.at[k], (above, slab))

    def back_copy(k):
        return remote(visit_sum.at[k], returned.at[k], send_back.at[k], recv_back.at[k], (below, slab))

    def down_copy(p):
        return remote(down_out.at[p], down_in.at[p], send_down.at[p], recv_down.at[p], (band, slab + 1))

    def up_copy(p):
        return remote(up_out.at[p], up_in.at[p], send_up.at[p], recv_up.at[p], (band, slab - 1))

    weight_copy = remote(weight_out, weight_in, send_weight, recv_weight, (above, slab))
    for k in range(members):
        orb_copy(k).start()
    weight_copy.start()

    diagonal = diagonal_ref[...]
    pivot = 1.0 / diagonal
    pivots[0] = pivot
    for z in range(1, planes):
        pivot = 1.0 / (diagonal - pivot)
        pivots[z] = pivot
    response = pivot
    reach[planes - 1] = response
    for z in range(planes - 2, -1, -1):
        response = response * pivots[z]
        reach[z] = response
    near, far = pivot, response

    def closing(count):
        def step(_, value):
            return near + far * far * value / (1.0 - value * near)
        return lax.fori_loop(0, count, step, jnp.zeros_like(near))

    close_left = closing(slab)
    close_right = closing(slabs - 1 - slab)
    gap_left = 1.0 - close_left * near
    gap_right = 1.0 - close_right * near
    scale = 1.0 / (gap_left * gap_right - close_left * close_right * far * far)
    coefs[0] = close_left
    coefs[1] = close_right
    coefs[2] = far / gap_left
    coefs[3] = far / gap_right
    coefs[4] = gap_right * scale
    coefs[5] = close_left * far * scale
    coefs[6] = gap_left * scale
    coefs[7] = close_right * far * scale

    @pl.loop(0, members)
    def _(k):
        @pl.loop(0, planes)
        def _(z):
            zero = jnp.zeros((points, points), jnp.float32)
            out[k, z] = zero
            visit_sum[k, z] = zero

    @pl.when(first)
    def _():
        @pl.loop(0, pairs)
        def _(p):
            down_in[p] = jnp.zeros((points, points), jnp.float32)

    @pl.when(last)
    def _():
        @pl.loop(0, pairs)
        def _(p):
            up_in[p] = jnp.zeros((points, points), jnp.float32)

    weight_copy.wait()

    def forward(p):
        j, i = p // members, lax.rem(p, members)

        def step(h, carry):
            z = 2 * h
            one, two = plane_pair(
                orbitals[i, z] * visitors[j, z],
                orbitals[i, z + 1] * visitors[j, z + 1],
                right_ref[...], left_ref[...],
            )
            one = (one + carry) * pivots[z]
            spectra[p, z] = one
            two = (two + one) * pivots[z + 1]
            spectra[p, z + 1] = two
            return two

        value = lax.fori_loop(0, planes // 2, step, jnp.zeros((points, points), jnp.float32), unroll=2)

        def back(h, value):
            z = planes - 2 - h
            value = spectra[p, z] + pivots[z] * value
            spectra[p, z] = value
            return value

        lax.fori_loop(0, planes - 1, back, value)

    def relay_down(p):
        @pl.when(jnp.logical_not(first))
        def _():
            down_copy(p).wait_recv()

        @pl.when(jnp.logical_not(last))
        def _():
            down_out[p] = spectra[p, planes - 1] + coefs[2] * (down_in[p] + coefs[0] * spectra[p, 0])
            down_copy(p).start()

    def relay_up(p):
        @pl.when(jnp.logical_not(last))
        def _():
            up_copy(p).wait_recv()

        @pl.when(jnp.logical_not(first))
        def _():
            up_out[p] = spectra[p, 0] + coefs[3] * (up_in[p] + coefs[1] * spectra[p, planes - 1])
            up_copy(p).start()

    def inverse(p):
        j, i = p // members, lax.rem(p, members)
        from_left = down_in[p] + coefs[0] * spectra[p, 0]
        from_right = up_in[p] + coefs[1] * spectra[p, planes - 1]
        coefs[8] = coefs[4] * from_left + coefs[5] * from_right
        coefs[9] = coefs[6] * from_right + coefs[7] * from_left
        planned = live[i, below * members + j].astype(jnp.float32)
        own_weight = occupation[assignment[i]]
        own_factor = weight_in[j, 0:1, :] * (-planned)
        visit_factor = -(planned * own_weight)

        @pl.loop(0, planes // 2, unroll=2)
        def _(h):
            z = 2 * h
            one = spectra[p, z] + reach[planes - 1 - z] * coefs[8] + reach[z] * coefs[9]
            two = spectra[p, z + 1] + reach[planes - 2 - z] * coefs[8] + reach[z + 1] * coefs[9]
            one, two = plane_pair(one, two, right_ref[...], left_ref[...])
            for y, value in ((z, one), (z + 1, two)):
                out[i, y] += own_factor * (value * visitors[j, y])
                visit_sum[j, y] += visit_factor * (value * orbitals[i, y])

    @pl.loop(0, pairs + slabs - 1)
    def _(t):
        @pl.when(t < pairs)
        def _():
            @pl.when(lax.rem(t, members) == 0)
            def _():
                orb_copy(t // members).wait_recv()

            forward(t)

        down = t - slab

        @pl.when(jnp.logical_and(down >= 0, down < pairs))
        def _():
            relay_down(down)

        up = t - (slabs - 1 - slab)

        @pl.when(jnp.logical_and(up >= 0, up < pairs))
        def _():
            relay_up(up)

        ready = t - (slabs - 1)

        @pl.when(ready >= 0)
        def _():
            inverse(ready)

            @pl.when(lax.rem(ready, members) == members - 1)
            def _():
                back_copy(ready // members).start()

    for k in range(members):
        back_copy(k).wait_recv()

        @pl.loop(0, planes)
        def _(z):
            out[k, z] += returned[k, z]

    for k in range(members):
        orb_copy(k).wait_send()
        back_copy(k).wait_send()

    @pl.when(jnp.logical_not(last))
    def _():
        @pl.loop(0, pairs)
        def _(p):
            down_copy(p).wait_send()

    @pl.when(jnp.logical_not(first))
    def _():
        @pl.loop(0, pairs)
        def _(p):
            up_copy(p).wait_send()


def local(bands, slabs, orbitals, occupation, assignment, pair_live):
    members, planes, points, _ = orbitals.shape
    pairs = members * members
    right, left, diagonal = tables(points)
    vmem = pl.BlockSpec(memory_space=pltpu.VMEM)
    smem = pl.BlockSpec(memory_space=pltpu.SMEM)
    block = pltpu.VMEM((members, planes, points, points), jnp.float32)
    faces = pltpu.VMEM((pairs, points, points), jnp.float32)
    column = pltpu.VMEM((planes, points, points), jnp.float32)
    dma = pltpu.SemaphoreType.DMA
    return pl.pallas_call(
        functools.partial(kernel, bands, slabs),
        out_shape=jax.ShapeDtypeStruct(orbitals.shape, jnp.float32),
        in_specs=[vmem, smem, smem, smem, vmem, vmem, vmem],
        out_specs=vmem,
        scratch_shapes=[
            block, block, block,
            pltpu.VMEM((pairs, planes, points, points), jnp.float32),
            faces, faces, faces, faces,
            column, column,
            pltpu.VMEM((10, points, points), jnp.float32),
            pltpu.VMEM((members, 8, points), jnp.float32),
            pltpu.VMEM((members, 8, points), jnp.float32),
            dma((members,)), dma((members,)), dma, dma, dma((members,)), dma((members,)),
            dma((pairs,)), dma((pairs,)), dma((pairs,)), dma((pairs,)),
        ],
        compiler_params=pltpu.CompilerParams(
            collective_id=0, has_side_effects=True, vmem_limit_bytes=60000 * 1024
        ),
    )(
        orbitals, occupation, assignment, pair_live,
        jnp.asarray(right), jnp.asarray(left), jnp.asarray(diagonal),
    )


def solution(mesh):
    placed = (P("band", "slab", None, None), P(), P("band"), P("band", None))
    return jax.shard_map(
        functools.partial(local, mesh.shape["band"], mesh.shape["slab"]),
        mesh=mesh, in_specs=placed, out_specs=P("band", "slab", None, None), check_vma=False,
    )
```

```python
import functools

import jax
import jax.numpy as jnp
import numpy as np
from jax import lax
from jax.experimental import pallas as pl
from jax.experimental.pallas import tpu as pltpu
from jax.sharding import PartitionSpec as P

screening = 0.01
lateral = 0.01
MESH = pl.DeviceIdType.MESH


def tables(points):
    numbers = np.arange(points, dtype=np.float64) + 1.0
    sine = np.sqrt(2.0 / (points + 1.0)) * np.sin(
        np.pi * numbers[:, None] * numbers[None, :] / (points + 1.0)
    )
    eigen = 2.0 - 2.0 * np.cos(np.pi * numbers / (points + 1.0))
    sine = sine.astype(np.float32)
    high = sine.astype(jnp.bfloat16)
    low = (sine - high.astype(np.float32)).astype(jnp.bfloat16)
    half = np.concatenate([high, low], axis=1)
    right = np.concatenate([half, half], axis=0)
    diagonal = 2.0 + lateral * (eigen[:, None] + eigen[None, :]) + screening
    return right, np.ascontiguousarray(right.T), diagonal.astype(np.float32)


def split(value):
    high = value.astype(jnp.bfloat16)
    low = (value - high.astype(jnp.float32)).astype(jnp.bfloat16)
    return high, low


def plane_pair(first, second, right, left):
    points = first.shape[0]
    high, low = split(jnp.concatenate([first, second], axis=0))
    both = jnp.dot(
        jnp.concatenate([high, low], axis=1), right, preferred_element_type=jnp.float32
    )
    rows = both[:, :points] + both[:, points:]
    high, low = split(rows)
    stacked = jnp.concatenate(
        [
            jnp.concatenate([high[:points], high[points:]], axis=1),
            jnp.concatenate([low[:points], low[points:]], axis=1),
        ],
        axis=0,
    )
    both = jnp.dot(left, stacked, preferred_element_type=jnp.float32)
    result = both[:points] + both[points:]
    return result[:, :points], result[:, points:]


def kernel(
    bands, slabs,
    orbitals, occupation, assignment, live, right_ref, left_ref, diagonal_ref,
    out,
    visitors, visit_sum, returned, spectra, down_in, down_out, up_in, up_out,
    faces, face_out, edges, edge_out, merged,
    pivots, reach, coefs, bounds, weight_out, weight_in,
    send_orb, recv_orb, send_weight, recv_weight, send_back, recv_back,
    send_down, recv_down, send_up, recv_up, send_face, recv_face, send_edge, recv_edge,
):
    members, planes, points, _ = orbitals.shape
    pairs = members * members
    band = lax.axis_index("band")
    slab = lax.axis_index("slab")
    above = lax.rem(band + 1, bands)
    below = lax.rem(band + bands - 1, bands)
    side = lax.rem(slab, 2)
    partner = slab + 1 - 2 * side
    duo, duos = slab // 2, slabs // 2
    first, last = duo == 0, duo == duos - 1
    half = points // 2
    mine = pl.ds(pl.multiple_of(side * half, half), half)
    other = pl.ds(pl.multiple_of((1 - side) * half, half), half)

    barrier = pltpu.get_barrier_semaphore()
    for neighbour in (above, below):
        pl.semaphore_signal(barrier, inc=1, device_id=(neighbour, slab), device_id_type=MESH)
    pl.semaphore_signal(barrier, inc=1, device_id=(band, partner), device_id_type=MESH)

    @pl.when(jnp.logical_not(first))
    def _():
        pl.semaphore_signal(barrier, inc=1, device_id=(band, slab - 2), device_id_type=MESH)

    @pl.when(jnp.logical_not(last))
    def _():
        pl.semaphore_signal(barrier, inc=1, device_id=(band, slab + 2), device_id_type=MESH)

    weights = [occupation[assignment[k]] for k in range(members)]
    for k in range(members):
        weight_out[k] = jnp.full(weight_out.shape[1:], weights[k], jnp.float32)

    pl.semaphore_wait(barrier, 5 - first.astype(jnp.int32) - last.astype(jnp.int32))

    def remote(source, target, sent, landed, device):
        return pltpu.make_async_remote_copy(
            src_ref=source, dst_ref=target, send_sem=sent, recv_sem=landed,
            device_id=device, device_id_type=MESH,
        )

    def orb_copy(k):
        return remote(orbitals.at[k], visitors.at[k], send_orb.at[k], recv_orb.at[k], (above, slab))

    def back_copy(k):
        return remote(visit_sum.at[k], returned.at[k], send_back.at[k], recv_back.at[k], (below, slab))

    def down_copy(p):
        return remote(down_out.at[p], down_in.at[p], send_down.at[p], recv_down.at[p], (band, slab + 2))

    def up_copy(p):
        return remote(up_out.at[p], up_in.at[p], send_up.at[p], recv_up.at[p], (band, slab - 2))

    def face_copy(p):
        return remote(face_out.at[p], faces.at[p, side], send_face.at[p], recv_face.at[p], (band, partner))

    def edge_copy(p):
        return remote(edge_out.at[p], edges.at[p, side], send_edge.at[p], recv_edge.at[p], (band, partner))

    weight_copy = remote(weight_out, weight_in, send_weight, recv_weight, (above, slab))
    weight_copy.start()
    orb_copy(0).start()

    diagonal = diagonal_ref[...]
    pivot = 1.0 / diagonal
    pivots[0] = pivot
    for z in range(1, planes):
        pivot = 1.0 / (diagonal - pivot)
        pivots[z] = pivot
    response = pivot
    reach[planes - 1] = response
    for z in range(planes - 2, -1, -1):
        response = response * pivots[z]
        reach[z] = response
    near, far = reach[planes - 1, mine, :], reach[0, mine, :]
    inner = 1.0 / (1.0 - near * near)
    near_two = near + far * far * near * inner
    far_two = far * far * inner

    def closing(count):
        def step(_, value):
            return near_two + far_two * far_two * value / (1.0 - value * near_two)
        return lax.fori_loop(0, count, step, jnp.zeros_like(near))

    close_left = closing(duo)
    close_right = closing(duos - 1 - duo)
    gap_left = 1.0 - close_left * near_two
    gap_right = 1.0 - close_right * near_two
    scale = 1.0 / (gap_left * gap_right - close_left * close_right * far_two * far_two)
    coefs[0] = close_left
    coefs[1] = close_right
    coefs[2] = far_two / gap_left
    coefs[3] = far_two / gap_right
    coefs[4] = gap_right * scale
    coefs[5] = close_left * far_two * scale
    coefs[6] = gap_left * scale
    coefs[7] = close_right * far_two * scale
    coefs[8] = inner
    coefs[9] = near * inner
    coefs[10] = far

    @pl.loop(0, members)
    def _(k):
        @pl.loop(0, planes)
        def _(z):
            zero = jnp.zeros((points, points), jnp.float32)
            out[k, z] = zero
            visit_sum[k, z] = zero

    @pl.when(first)
    def _():
        @pl.loop(0, pairs)
        def _(p):
            down_in[p] = jnp.zeros((half, points), jnp.float32)

    @pl.when(last)
    def _():
        @pl.loop(0, pairs)
        def _(p):
            up_in[p] = jnp.zeros((half, points), jnp.float32)

    weight_copy.wait()

    def forward(p):
        j, i = p // members, lax.rem(p, members)

        def step(h, carry):
            z = 2 * h
            one, two = plane_pair(
                orbitals[i, z] * visitors[j, z],
                orbitals[i, z + 1] * visitors[j, z + 1],
                right_ref[...], left_ref[...],
            )
            one = (one + carry) * pivots[z]
            spectra[p, z] = one
            two = (two + one) * pivots[z + 1]
            spectra[p, z + 1] = two
            return two

        value = lax.fori_loop(0, planes // 2, step, jnp.zeros((points, points), jnp.float32), unroll=2)

        def back(h, value):
            z = planes - 2 - h
            value = spectra[p, z] + pivots[z] * value
            spectra[p, z] = value
            return value

        lax.fori_loop(0, planes - 1, back, value)
        for n, z in enumerate((0, planes - 1)):
            face_out[p, n] = spectra[p, z, other, :]
            faces[p, side, n] = spectra[p, z, mine, :]
        face_copy(p).start()

    def merge(p):
        face_copy(p).wait_recv()
        head, tail = faces[p, 0, 1], faces[p, 1, 0]
        merged[p, 0] = faces[p, 0, 0] + coefs[10] * (coefs[8] * tail + coefs[9] * head)
        merged[p, 1] = faces[p, 1, 1] + coefs[10] * (coefs[8] * head + coefs[9] * tail)

    def relay_down(p):
        @pl.when(jnp.logical_not(first))
        def _():
            down_copy(p).wait_recv()

        @pl.when(jnp.logical_not(last))
        def _():
            down_out[p] = merged[p, 1] + coefs[2] * (down_in[p] + coefs[0] * merged[p, 0])
            down_copy(p).start()

    def relay_up(p):
        @pl.when(jnp.logical_not(last))
        def _():
            up_copy(p).wait_recv()

        @pl.when(jnp.logical_not(first))
        def _():
            up_out[p] = merged[p, 0] + coefs[3] * (up_in[p] + coefs[1] * merged[p, 1])
            up_copy(p).start()

    def finish(p):
        from_left = down_in[p] + coefs[0] * merged[p, 0]
        from_right = up_in[p] + coefs[1] * merged[p, 1]
        beyond_left = coefs[4] * from_left + coefs[5] * from_right
        beyond_right = coefs[6] * from_right + coefs[7] * from_left
        head = faces[p, 0, 1] + coefs[10] * beyond_left
        tail = faces[p, 1, 0] + coefs[10] * beyond_right
        inner_left = coefs[8] * head + coefs[9] * tail
        inner_right = coefs[8] * tail + coefs[9] * head
        lower = side == 0
        edges[p, side, 0] = jnp.where(lower, beyond_left, inner_left)
        edges[p, side, 1] = jnp.where(lower, inner_right, beyond_right)
        edge_out[p, 0] = jnp.where(lower, inner_left, beyond_left)
        edge_out[p, 1] = jnp.where(lower, beyond_right, inner_right)
        edge_copy(p).start()

    def inverse(p):
        j, i = p // members, lax.rem(p, members)
        edge_copy(p).wait_recv()
        for n in range(2):
            bounds[n] = jnp.concatenate([edges[p, 0, n], edges[p, 1, n]], axis=0)
        planned = live[i, below * members + j].astype(jnp.float32)
        own_weight = occupation[assignment[i]]
        own_factor = weight_in[j, 0:1, :] * (-planned)
        visit_factor = -(planned * own_weight)

        @pl.loop(0, planes // 2, unroll=2)
        def _(h):
            z = 2 * h
            one = spectra[p, z] + reach[planes - 1 - z] * bounds[0] + reach[z] * bounds[1]
            two = spectra[p, z + 1] + reach[planes - 2 - z] * bounds[0] + reach[z + 1] * bounds[1]
            one, two = plane_pair(one, two, right_ref[...], left_ref[...])
            for y, value in ((z, one), (z + 1, two)):
                out[i, y] += own_factor * (value * visitors[j, y])
                visit_sum[j, y] += visit_factor * (value * orbitals[i, y])

    def within(p):
        return jnp.logical_and(p >= 0, p < pairs)

    @pl.loop(0, pairs + duos + 1)
    def _(t):
        joined = t - 1

        @pl.when(within(joined))
        def _():
            merge(joined)

        down = t - 1 - duo

        @pl.when(within(down))
        def _():
            relay_down(down)

        up = t - duos + duo

        @pl.when(within(up))
        def _():
            relay_up(up)

        closed = t - duos

        @pl.when(within(closed))
        def _():
            finish(closed)

        @pl.when(t < pairs)
        def _():
            @pl.when(lax.rem(t, members) == 0)
            def _():
                k = t // members
                orb_copy(k).wait()

                @pl.when(k < members - 1)
                def _():
                    orb_copy(k + 1).start()

            forward(t)

        ready = t - duos - 1

        @pl.when(ready >= 0)
        def _():
            inverse(ready)

            @pl.when(lax.rem(ready, members) == members - 1)
            def _():
                back_copy(ready // members).start()

    for k in range(members):
        back_copy(k).wait_recv()

        @pl.loop(0, planes)
        def _(z):
            out[k, z] += returned[k, z]

    for k in range(members):
        back_copy(k).wait_send()

    @pl.loop(0, pairs)
    def _(p):
        face_copy(p).wait_send()
        edge_copy(p).wait_send()

    @pl.when(jnp.logical_not(last))
    def _():
        @pl.loop(0, pairs)
        def _(p):
            down_copy(p).wait_send()

    @pl.when(jnp.logical_not(first))
    def _():
        @pl.loop(0, pairs)
        def _(p):
            up_copy(p).wait_send()


def local(bands, slabs, orbitals, occupation, assignment, pair_live):
    members, planes, points, _ = orbitals.shape
    pairs = members * members
    right, left, diagonal = tables(points)
    vmem = pl.BlockSpec(memory_space=pltpu.VMEM)
    smem = pl.BlockSpec(memory_space=pltpu.SMEM)
    block = pltpu.VMEM((members, planes, points, points), jnp.float32)
    half = pltpu.VMEM((pairs, points // 2, points), jnp.float32)
    twice = pltpu.VMEM((pairs, 2, points // 2, points), jnp.float32)
    quad = pltpu.VMEM((pairs, 2, 2, points // 2, points), jnp.float32)
    column = pltpu.VMEM((planes, points, points), jnp.float32)
    dma = pltpu.SemaphoreType.DMA
    return pl.pallas_call(
        functools.partial(kernel, bands, slabs),
        out_shape=jax.ShapeDtypeStruct(orbitals.shape, jnp.float32),
        in_specs=[vmem, smem, smem, smem, vmem, vmem, vmem],
        out_specs=vmem,
        scratch_shapes=[
            block, block, block,
            pltpu.VMEM((pairs, planes, points, points), jnp.float32),
            half, half, half, half,
            quad, twice, quad, twice, twice,
            column, column,
            pltpu.VMEM((11, points // 2, points), jnp.float32),
            pltpu.VMEM((2, points, points), jnp.float32),
            pltpu.VMEM((members, 8, points), jnp.float32),
            pltpu.VMEM((members, 8, points), jnp.float32),
            dma((members,)), dma((members,)), dma, dma, dma((members,)), dma((members,)),
            *[dma((pairs,)) for _ in range(8)],
        ],
        compiler_params=pltpu.CompilerParams(
            collective_id=0, has_side_effects=True, vmem_limit_bytes=60000 * 1024
        ),
    )(
        orbitals, occupation, assignment, pair_live,
        jnp.asarray(right), jnp.asarray(left), jnp.asarray(diagonal),
    )


def solution(mesh):
    placed = (P("band", "slab", None, None), P(), P("band"), P("band", None))
    return jax.shard_map(
        functools.partial(local, mesh.shape["band"], mesh.shape["slab"]),
        mesh=mesh, in_specs=placed, out_specs=P("band", "slab", None, None), check_vma=False,
    )
```

```python
import functools

import jax
import jax.numpy as jnp
import numpy as np
from jax import lax
from jax.experimental import pallas as pl
from jax.experimental.pallas import tpu as pltpu
from jax.sharding import PartitionSpec as P

screening = 0.01
lateral = 0.01
MESH = pl.DeviceIdType.MESH
gap = 0


def tables(points):
    numbers = np.arange(points, dtype=np.float64) + 1.0
    sine = np.sqrt(2.0 / (points + 1.0)) * np.sin(
        np.pi * numbers[:, None] * numbers[None, :] / (points + 1.0)
    )
    eigen = 2.0 - 2.0 * np.cos(np.pi * numbers / (points + 1.0))
    sine = sine.astype(np.float32)
    high = sine.astype(jnp.bfloat16)
    low = (sine - high.astype(np.float32)).astype(jnp.bfloat16)
    half = np.concatenate([high, low], axis=1)
    right = np.concatenate([half, half], axis=0)
    diagonal = 2.0 + lateral * (eigen[:, None] + eigen[None, :]) + screening
    return right, np.ascontiguousarray(right.T), diagonal.astype(np.float32)


def split(value):
    high = value.astype(jnp.bfloat16)
    low = (value - high.astype(jnp.float32)).astype(jnp.bfloat16)
    return high, low


def plane_pair(first, second, right, left):
    points = first.shape[0]
    high, low = split(jnp.concatenate([first, second], axis=0))
    both = jnp.dot(
        jnp.concatenate([high, low], axis=1), right, preferred_element_type=jnp.float32
    )
    rows = both[:, :points] + both[:, points:]
    high, low = split(rows)
    stacked = jnp.concatenate(
        [
            jnp.concatenate([high[:points], high[points:]], axis=1),
            jnp.concatenate([low[:points], low[points:]], axis=1),
        ],
        axis=0,
    )
    both = jnp.dot(left, stacked, preferred_element_type=jnp.float32)
    result = both[:points] + both[points:]
    return result[:, :points], result[:, points:]


def kernel(
    bands, slabs,
    orbitals, occupation, assignment, live, right_ref, left_ref, diagonal_ref,
    out,
    visitors, visit_sum, returned, spectra, down_in, down_out, up_in, up_out,
    faces, face_out, edges, edge_out, merged,
    pivots, reach, coefs, bounds, weight_out, weight_in,
    send_orb, recv_orb, send_weight, recv_weight, send_back, recv_back,
    send_down, recv_down, send_up, recv_up, send_face, recv_face, send_edge, recv_edge,
):
    members, planes, points, _ = orbitals.shape
    pairs = members * members
    band = lax.axis_index("band")
    slab = lax.axis_index("slab")
    above = lax.rem(band + 1, bands)
    below = lax.rem(band + bands - 1, bands)
    side = lax.rem(slab, 2)
    partner = slab + 1 - 2 * side
    duo, duos = slab // 2, slabs // 2
    first, last = duo == 0, duo == duos - 1
    half = points // 2
    mine = pl.ds(pl.multiple_of(side * half, half), half)
    other = pl.ds(pl.multiple_of((1 - side) * half, half), half)

    barrier = pltpu.get_barrier_semaphore()
    for neighbour in (above, below):
        pl.semaphore_signal(barrier, inc=1, device_id=(neighbour, slab), device_id_type=MESH)
    pl.semaphore_signal(barrier, inc=1, device_id=(band, partner), device_id_type=MESH)

    @pl.when(jnp.logical_not(first))
    def _():
        pl.semaphore_signal(barrier, inc=1, device_id=(band, slab - 2), device_id_type=MESH)

    @pl.when(jnp.logical_not(last))
    def _():
        pl.semaphore_signal(barrier, inc=1, device_id=(band, slab + 2), device_id_type=MESH)

    weights = [occupation[assignment[k]] for k in range(members)]
    for k in range(members):
        weight_out[k] = jnp.full(weight_out.shape[1:], weights[k], jnp.float32)

    pl.semaphore_wait(barrier, 5 - first.astype(jnp.int32) - last.astype(jnp.int32))

    def remote(source, target, sent, landed, device):
        return pltpu.make_async_remote_copy(
            src_ref=source, dst_ref=target, send_sem=sent, recv_sem=landed,
            device_id=device, device_id_type=MESH,
        )

    def orb_copy(k):
        return remote(orbitals.at[k], visitors.at[k], send_orb.at[k], recv_orb.at[k], (above, slab))

    def back_copy(k):
        return remote(visit_sum.at[k], returned.at[k], send_back.at[k], recv_back.at[k], (below, slab))

    def down_copy(p):
        return remote(down_out.at[p], down_in.at[p], send_down.at[p], recv_down.at[p], (band, slab + 2))

    def up_copy(p):
        return remote(up_out.at[p], up_in.at[p], send_up.at[p], recv_up.at[p], (band, slab - 2))

    def face_copy(p):
        return remote(face_out.at[p], faces.at[p, side], send_face.at[p], recv_face.at[p], (band, partner))

    def edge_copy(p):
        return remote(edge_out.at[p], edges.at[p, side], send_edge.at[p], recv_edge.at[p], (band, partner))

    weight_copy = remote(weight_out, weight_in, send_weight, recv_weight, (above, slab))
    weight_copy.start()
    orb_copy(0).start()

    diagonal = diagonal_ref[...]
    pivot = 1.0 / diagonal
    pivots[0] = pivot
    for z in range(1, planes):
        pivot = 1.0 / (diagonal - pivot)
        pivots[z] = pivot
    response = pivot
    reach[planes - 1] = response
    for z in range(planes - 2, -1, -1):
        response = response * pivots[z]
        reach[z] = response
    near, far = reach[planes - 1, mine, :], reach[0, mine, :]
    inner = 1.0 / (1.0 - near * near)
    near_two = near + far * far * near * inner
    far_two = far * far * inner

    def closing(count):
        def step(_, value):
            return near_two + far_two * far_two * value / (1.0 - value * near_two)
        return lax.fori_loop(0, count, step, jnp.zeros_like(near))

    close_left = closing(duo)
    close_right = closing(duos - 1 - duo)
    gap_left = 1.0 - close_left * near_two
    gap_right = 1.0 - close_right * near_two
    scale = 1.0 / (gap_left * gap_right - close_left * close_right * far_two * far_two)
    coefs[0] = close_left
    coefs[1] = close_right
    coefs[2] = far_two / gap_left
    coefs[3] = far_two / gap_right
    coefs[4] = gap_right * scale
    coefs[5] = close_left * far_two * scale
    coefs[6] = gap_left * scale
    coefs[7] = close_right * far_two * scale
    coefs[8] = inner
    coefs[9] = near * inner
    coefs[10] = far

    @pl.loop(0, members)
    def _(k):
        @pl.loop(0, planes)
        def _(z):
            zero = jnp.zeros((points, points), jnp.float32)
            out[k, z] = zero
            visit_sum[k, z] = zero

    @pl.when(first)
    def _():
        @pl.loop(0, pairs)
        def _(p):
            down_in[p] = jnp.zeros((half, points), jnp.float32)

    @pl.when(last)
    def _():
        @pl.loop(0, pairs)
        def _(p):
            up_in[p] = jnp.zeros((half, points), jnp.float32)

    weight_copy.wait()

    def forward(p):
        j, i = p // members, lax.rem(p, members)

        def step(h, carry):
            z = 2 * h
            one, two = plane_pair(
                orbitals[i, z] * visitors[j, z],
                orbitals[i, z + 1] * visitors[j, z + 1],
                right_ref[...], left_ref[...],
            )
            one = (one + carry) * pivots[z]
            spectra[p, z] = one
            two = (two + one) * pivots[z + 1]
            spectra[p, z + 1] = two
            return two

        value = lax.fori_loop(0, planes // 2, step, jnp.zeros((points, points), jnp.float32), unroll=2)

        def back(h, value):
            z = planes - 2 - h
            value = spectra[p, z] + pivots[z] * value
            spectra[p, z] = value
            return value

        lax.fori_loop(0, planes - 1, back, value)
        for n, z in enumerate((0, planes - 1)):
            face_out[p, n] = spectra[p, z, other, :]
            faces[p, side, n] = spectra[p, z, mine, :]
        face_copy(p).start()

    def merge(p):
        face_copy(p).wait_recv()
        head, tail = faces[p, 0, 1], faces[p, 1, 0]
        merged[p, 0] = faces[p, 0, 0] + coefs[10] * (coefs[8] * tail + coefs[9] * head)
        merged[p, 1] = faces[p, 1, 1] + coefs[10] * (coefs[8] * head + coefs[9] * tail)

    def relay_down(p):
        @pl.when(jnp.logical_not(first))
        def _():
            down_copy(p).wait_recv()

        @pl.when(jnp.logical_not(last))
        def _():
            down_out[p] = merged[p, 1] + coefs[2] * (down_in[p] + coefs[0] * merged[p, 0])
            down_copy(p).start()

    def relay_up(p):
        @pl.when(jnp.logical_not(last))
        def _():
            up_copy(p).wait_recv()

        @pl.when(jnp.logical_not(first))
        def _():
            up_out[p] = merged[p, 0] + coefs[3] * (up_in[p] + coefs[1] * merged[p, 1])
            up_copy(p).start()

    def finish(p):
        from_left = down_in[p] + coefs[0] * merged[p, 0]
        from_right = up_in[p] + coefs[1] * merged[p, 1]
        beyond_left = coefs[4] * from_left + coefs[5] * from_right
        beyond_right = coefs[6] * from_right + coefs[7] * from_left
        head = faces[p, 0, 1] + coefs[10] * beyond_left
        tail = faces[p, 1, 0] + coefs[10] * beyond_right
        inner_left = coefs[8] * head + coefs[9] * tail
        inner_right = coefs[8] * tail + coefs[9] * head
        lower = side == 0
        edges[p, side, 0] = jnp.where(lower, beyond_left, inner_left)
        edges[p, side, 1] = jnp.where(lower, inner_right, beyond_right)
        edge_out[p, 0] = jnp.where(lower, inner_left, beyond_left)
        edge_out[p, 1] = jnp.where(lower, beyond_right, inner_right)
        edge_copy(p).start()

    def inverse(p):
        j, i = p // members, lax.rem(p, members)
        edge_copy(p).wait_recv()
        for n in range(2):
            bounds[n] = jnp.concatenate([edges[p, 0, n], edges[p, 1, n]], axis=0)
        planned = live[i, below * members + j].astype(jnp.float32)
        own_weight = occupation[assignment[i]]
        own_factor = weight_in[j, 0:1, :] * (-planned)
        visit_factor = -(planned * own_weight)

        @pl.loop(0, planes // 2, unroll=2)
        def _(h):
            z = 2 * h
            one = spectra[p, z] + reach[planes - 1 - z] * bounds[0] + reach[z] * bounds[1]
            two = spectra[p, z + 1] + reach[planes - 2 - z] * bounds[0] + reach[z + 1] * bounds[1]
            one, two = plane_pair(one, two, right_ref[...], left_ref[...])
            for y, value in ((z, one), (z + 1, two)):
                out[i, y] += own_factor * (value * visitors[j, y])
                visit_sum[j, y] += visit_factor * (value * orbitals[i, y])

    group = members + gap

    def planned_at(slot, stage):
        count = lax.div(jnp.maximum(slot, 0), group)
        member = lax.rem(jnp.maximum(slot, 0), group)
        inside = jnp.logical_and(slot >= 0, jnp.logical_and(member < members, count < members))

        @pl.when(inside)
        def _():
            stage(count, member, count * members + member)

    def enter(k, i, p):
        @pl.when(i == 0)
        def _():
            orb_copy(k).wait()

            @pl.when(k < members - 1)
            def _():
                orb_copy(k + 1).start()

        forward(p)

    def leave(k, i, p):
        inverse(p)

        @pl.when(i == members - 1)
        def _():
            back_copy(k).start()

    @pl.loop(0, members * group - gap + duos + 1)
    def _(t):
        planned_at(t, enter)
        planned_at(t - 1, lambda k, i, p: merge(p))
        planned_at(t - 1 - duo, lambda k, i, p: relay_down(p))
        planned_at(t - duos + duo, lambda k, i, p: relay_up(p))
        planned_at(t - duos, lambda k, i, p: finish(p))
        planned_at(t - duos - 1, leave)

    for k in range(members):
        back_copy(k).wait_recv()

        @pl.loop(0, planes)
        def _(z):
            out[k, z] += returned[k, z]

    for k in range(members):
        back_copy(k).wait_send()

    @pl.loop(0, pairs)
    def _(p):
        face_copy(p).wait_send()
        edge_copy(p).wait_send()

    @pl.when(jnp.logical_not(last))
    def _():
        @pl.loop(0, pairs)
        def _(p):
            down_copy(p).wait_send()

    @pl.when(jnp.logical_not(first))
    def _():
        @pl.loop(0, pairs)
        def _(p):
            up_copy(p).wait_send()


def local(bands, slabs, orbitals, occupation, assignment, pair_live):
    members, planes, points, _ = orbitals.shape
    pairs = members * members
    right, left, diagonal = tables(points)
    vmem = pl.BlockSpec(memory_space=pltpu.VMEM)
    smem = pl.BlockSpec(memory_space=pltpu.SMEM)
    block = pltpu.VMEM((members, planes, points, points), jnp.float32)
    half = pltpu.VMEM((pairs, points // 2, points), jnp.float32)
    twice = pltpu.VMEM((pairs, 2, points // 2, points), jnp.float32)
    quad = pltpu.VMEM((pairs, 2, 2, points // 2, points), jnp.float32)
    column = pltpu.VMEM((planes, points, points), jnp.float32)
    dma = pltpu.SemaphoreType.DMA
    return pl.pallas_call(
        functools.partial(kernel, bands, slabs),
        out_shape=jax.ShapeDtypeStruct(orbitals.shape, jnp.float32),
        in_specs=[vmem, smem, smem, smem, vmem, vmem, vmem],
        out_specs=vmem,
        scratch_shapes=[
            block, block, block,
            pltpu.VMEM((pairs, planes, points, points), jnp.float32),
            half, half, half, half,
            quad, twice, quad, twice, twice,
            column, column,
            pltpu.VMEM((11, points // 2, points), jnp.float32),
            pltpu.VMEM((2, points, points), jnp.float32),
            pltpu.VMEM((members, 8, points), jnp.float32),
            pltpu.VMEM((members, 8, points), jnp.float32),
            dma((members,)), dma((members,)), dma, dma, dma((members,)), dma((members,)),
            *[dma((pairs,)) for _ in range(8)],
        ],
        compiler_params=pltpu.CompilerParams(
            collective_id=0, has_side_effects=True, vmem_limit_bytes=60000 * 1024
        ),
    )(
        orbitals, occupation, assignment, pair_live,
        jnp.asarray(right), jnp.asarray(left), jnp.asarray(diagonal),
    )


def solution(mesh):
    placed = (P("band", "slab", None, None), P(), P("band"), P("band", None))
    return jax.shard_map(
        functools.partial(local, mesh.shape["band"], mesh.shape["slab"]),
        mesh=mesh, in_specs=placed, out_specs=P("band", "slab", None, None), check_vma=False,
    )
```

```python
import functools

import jax
import jax.numpy as jnp
import numpy as np
from jax import lax
from jax.experimental import pallas as pl
from jax.experimental.pallas import tpu as pltpu
from jax.sharding import PartitionSpec as P

screening = 0.01
lateral = 0.01
MESH = pl.DeviceIdType.MESH
gap = 0


def tables(points):
    numbers = np.arange(points, dtype=np.float64) + 1.0
    sine = np.sqrt(2.0 / (points + 1.0)) * np.sin(
        np.pi * numbers[:, None] * numbers[None, :] / (points + 1.0)
    )
    eigen = 2.0 - 2.0 * np.cos(np.pi * numbers / (points + 1.0))
    sine = sine.astype(np.float32)
    high = sine.astype(jnp.bfloat16)
    low = (sine - high.astype(np.float32)).astype(jnp.bfloat16)
    half = np.concatenate([high, low], axis=1)
    right = np.concatenate([half, half], axis=0)
    diagonal = 2.0 + lateral * (eigen[:, None] + eigen[None, :]) + screening
    return right, np.ascontiguousarray(right.T), diagonal.astype(np.float32)


def split(value):
    high = value.astype(jnp.bfloat16)
    low = (value - high.astype(jnp.float32)).astype(jnp.bfloat16)
    return high, low


def plane_pair(first, second, right, left):
    points = first.shape[0]
    high, low = split(jnp.concatenate([first, second], axis=0))
    both = jnp.dot(
        jnp.concatenate([high, low], axis=1), right, preferred_element_type=jnp.float32
    )
    rows = both[:, :points] + both[:, points:]
    high, low = split(rows)
    stacked = jnp.concatenate(
        [
            jnp.concatenate([high[:points], high[points:]], axis=1),
            jnp.concatenate([low[:points], low[points:]], axis=1),
        ],
        axis=0,
    )
    both = jnp.dot(left, stacked, preferred_element_type=jnp.float32)
    result = both[:points] + both[points:]
    return result[:, :points], result[:, points:]


def kernel(
    bands, slabs,
    orbitals_hbm, occupation, assignment, live, right_ref, left_ref, diagonal_ref,
    out_hbm,
    orbitals, out, visitors, visit_sum, returned, spectra, down_in, down_out, up_in, up_out,
    faces, face_out, edges, edge_out, merged,
    pivots, reach, coefs, bounds, weight_out, weight_in,
    send_orb, recv_orb, send_weight, recv_weight, send_back, recv_back,
    send_down, recv_down, send_up, recv_up, send_face, recv_face, send_edge, recv_edge,
    load_sem, store_sem,
):
    members, planes, points, _ = orbitals_hbm.shape
    pairs = members * members
    load = pltpu.make_async_copy(orbitals_hbm, orbitals, load_sem)
    load.start()
    band = lax.axis_index("band")
    slab = lax.axis_index("slab")
    above = lax.rem(band + 1, bands)
    below = lax.rem(band + bands - 1, bands)
    side = lax.rem(slab, 2)
    partner = slab + 1 - 2 * side
    duo, duos = slab // 2, slabs // 2
    first, last = duo == 0, duo == duos - 1
    half = points // 2
    mine = pl.ds(pl.multiple_of(side * half, half), half)
    other = pl.ds(pl.multiple_of((1 - side) * half, half), half)

    barrier = pltpu.get_barrier_semaphore()
    for neighbour in (above, below):
        pl.semaphore_signal(barrier, inc=1, device_id=(neighbour, slab), device_id_type=MESH)
    pl.semaphore_signal(barrier, inc=1, device_id=(band, partner), device_id_type=MESH)

    @pl.when(jnp.logical_not(first))
    def _():
        pl.semaphore_signal(barrier, inc=1, device_id=(band, slab - 2), device_id_type=MESH)

    @pl.when(jnp.logical_not(last))
    def _():
        pl.semaphore_signal(barrier, inc=1, device_id=(band, slab + 2), device_id_type=MESH)

    weights = [occupation[assignment[k]] for k in range(members)]
    for k in range(members):
        weight_out[k] = jnp.full(weight_out.shape[1:], weights[k], jnp.float32)

    pl.semaphore_wait(barrier, 5 - first.astype(jnp.int32) - last.astype(jnp.int32))

    def remote(source, target, sent, landed, device):
        return pltpu.make_async_remote_copy(
            src_ref=source, dst_ref=target, send_sem=sent, recv_sem=landed,
            device_id=device, device_id_type=MESH,
        )

    def orb_copy(k):
        return remote(orbitals_hbm.at[k], visitors.at[k], send_orb.at[k], recv_orb.at[k], (above, slab))

    def back_copy(k, part):
        span = pl.ds(part * (planes // 2), planes // 2)
        return remote(
            visit_sum.at[k, span], returned.at[k, span],
            send_back.at[k, part], recv_back.at[k, part], (below, slab),
        )

    def down_copy(p):
        return remote(down_out.at[p], down_in.at[p], send_down.at[p], recv_down.at[p], (band, slab + 2))

    def up_copy(p):
        return remote(up_out.at[p], up_in.at[p], send_up.at[p], recv_up.at[p], (band, slab - 2))

    def face_copy(p):
        return remote(face_out.at[p], faces.at[p, side], send_face.at[p], recv_face.at[p], (band, partner))

    def edge_copy(p):
        return remote(edge_out.at[p], edges.at[p, side], send_edge.at[p], recv_edge.at[p], (band, partner))

    weight_copy = remote(weight_out, weight_in, send_weight, recv_weight, (above, slab))
    weight_copy.start()
    orb_copy(0).start()

    diagonal = diagonal_ref[...]
    pivot = 1.0 / diagonal
    pivots[0] = pivot
    for z in range(1, planes):
        pivot = 1.0 / (diagonal - pivot)
        pivots[z] = pivot
    response = pivot
    reach[planes - 1] = response
    for z in range(planes - 2, -1, -1):
        response = response * pivots[z]
        reach[z] = response
    near, far = reach[planes - 1, mine, :], reach[0, mine, :]
    inner = 1.0 / (1.0 - near * near)
    near_two = near + far * far * near * inner
    far_two = far * far * inner

    def closing(count):
        def step(_, value):
            return near_two + far_two * far_two * value / (1.0 - value * near_two)
        return lax.fori_loop(0, count, step, jnp.zeros_like(near))

    close_left = closing(duo)
    close_right = closing(duos - 1 - duo)
    gap_left = 1.0 - close_left * near_two
    gap_right = 1.0 - close_right * near_two
    scale = 1.0 / (gap_left * gap_right - close_left * close_right * far_two * far_two)
    coefs[0] = close_left
    coefs[1] = close_right
    coefs[2] = far_two / gap_left
    coefs[3] = far_two / gap_right
    coefs[4] = gap_right * scale
    coefs[5] = close_left * far_two * scale
    coefs[6] = gap_left * scale
    coefs[7] = close_right * far_two * scale
    coefs[8] = inner
    coefs[9] = near * inner
    coefs[10] = far

    @pl.loop(0, members)
    def _(k):
        @pl.loop(0, planes)
        def _(z):
            zero = jnp.zeros((points, points), jnp.float32)
            out[k, z] = zero
            visit_sum[k, z] = zero

    @pl.when(first)
    def _():
        @pl.loop(0, pairs)
        def _(p):
            down_in[p] = jnp.zeros((half, points), jnp.float32)

    @pl.when(last)
    def _():
        @pl.loop(0, pairs)
        def _(p):
            up_in[p] = jnp.zeros((half, points), jnp.float32)

    weight_copy.wait()
    load.wait()

    def forward(p):
        j, i = p // members, lax.rem(p, members)

        def step(h, carry):
            z = 2 * h
            one, two = plane_pair(
                orbitals[i, z] * visitors[j, z],
                orbitals[i, z + 1] * visitors[j, z + 1],
                right_ref[...], left_ref[...],
            )
            one = (one + carry) * pivots[z]
            spectra[p, z] = one
            two = (two + one) * pivots[z + 1]
            spectra[p, z + 1] = two
            return two

        value = lax.fori_loop(0, planes // 2, step, jnp.zeros((points, points), jnp.float32), unroll=min(4, planes // 2))

        def back(h, value):
            z = planes - 2 - h
            value = spectra[p, z] + pivots[z] * value
            spectra[p, z] = value
            return value

        lax.fori_loop(0, planes - 1, back, value)
        for n, z in enumerate((0, planes - 1)):
            face_out[p, n] = spectra[p, z, other, :]
            faces[p, side, n] = spectra[p, z, mine, :]
        face_copy(p).start()

    def merge(p):
        face_copy(p).wait_recv()
        head, tail = faces[p, 0, 1], faces[p, 1, 0]
        merged[p, 0] = faces[p, 0, 0] + coefs[10] * (coefs[8] * tail + coefs[9] * head)
        merged[p, 1] = faces[p, 1, 1] + coefs[10] * (coefs[8] * head + coefs[9] * tail)

    def relay_down(p):
        @pl.when(jnp.logical_not(first))
        def _():
            down_copy(p).wait_recv()

        @pl.when(jnp.logical_not(last))
        def _():
            down_out[p] = merged[p, 1] + coefs[2] * (down_in[p] + coefs[0] * merged[p, 0])
            down_copy(p).start()

    def relay_up(p):
        @pl.when(jnp.logical_not(last))
        def _():
            up_copy(p).wait_recv()

        @pl.when(jnp.logical_not(first))
        def _():
            up_out[p] = merged[p, 0] + coefs[3] * (up_in[p] + coefs[1] * merged[p, 1])
            up_copy(p).start()

    def finish(p):
        from_left = down_in[p] + coefs[0] * merged[p, 0]
        from_right = up_in[p] + coefs[1] * merged[p, 1]
        beyond_left = coefs[4] * from_left + coefs[5] * from_right
        beyond_right = coefs[6] * from_right + coefs[7] * from_left
        head = faces[p, 0, 1] + coefs[10] * beyond_left
        tail = faces[p, 1, 0] + coefs[10] * beyond_right
        inner_left = coefs[8] * head + coefs[9] * tail
        inner_right = coefs[8] * tail + coefs[9] * head
        lower = side == 0
        edges[p, side, 0] = jnp.where(lower, beyond_left, inner_left)
        edges[p, side, 1] = jnp.where(lower, inner_right, beyond_right)
        edge_out[p, 0] = jnp.where(lower, inner_left, beyond_left)
        edge_out[p, 1] = jnp.where(lower, beyond_right, inner_right)
        edge_copy(p).start()

    def inverse(p):
        j, i = p // members, lax.rem(p, members)
        edge_copy(p).wait_recv()
        for n in range(2):
            bounds[n] = jnp.concatenate([edges[p, 0, n], edges[p, 1, n]], axis=0)
        planned = live[i, below * members + j].astype(jnp.float32)
        own_weight = occupation[assignment[i]]
        own_factor = weight_in[j, 0:1, :] * (-planned)
        visit_factor = -(planned * own_weight)

        for part in range(2):
            @pl.loop(part * (planes // 4), (part + 1) * (planes // 4), unroll=min(4, planes // 4))
            def _(h):
                z = 2 * h
                one = spectra[p, z] + reach[planes - 1 - z] * bounds[0] + reach[z] * bounds[1]
                two = spectra[p, z + 1] + reach[planes - 2 - z] * bounds[0] + reach[z + 1] * bounds[1]
                one, two = plane_pair(one, two, right_ref[...], left_ref[...])
                for y, value in ((z, one), (z + 1, two)):
                    out[i, y] += own_factor * (value * visitors[j, y])
                    visit_sum[j, y] += visit_factor * (value * orbitals[i, y])

            @pl.when(i == members - 1)
            def _():
                back_copy(j, part).start()

    group = members + gap

    def planned_at(slot, stage):
        count = lax.div(jnp.maximum(slot, 0), group)
        member = lax.rem(jnp.maximum(slot, 0), group)
        inside = jnp.logical_and(slot >= 0, jnp.logical_and(member < members, count < members))

        @pl.when(inside)
        def _():
            stage(count, member, count * members + member)

    def enter(k, i, p):
        @pl.when(i == 0)
        def _():
            orb_copy(k).wait()

            @pl.when(k < members - 1)
            def _():
                orb_copy(k + 1).start()

        forward(p)

    def leave(k, i, p):
        inverse(p)

    @pl.loop(0, members * group - gap + duos + 1)
    def _(t):
        planned_at(t, enter)
        planned_at(t - 1, lambda k, i, p: merge(p))
        planned_at(t - 1 - duo, lambda k, i, p: relay_down(p))
        planned_at(t - duos + duo, lambda k, i, p: relay_up(p))
        planned_at(t - duos, lambda k, i, p: finish(p))
        planned_at(t - duos - 1, leave)

    def store(k):
        return pltpu.make_async_copy(out.at[k], out_hbm.at[k], store_sem.at[k])

    for k in range(members):
        for part in range(2):
            back_copy(k, part).wait_recv()

            @pl.loop(part * (planes // 2), (part + 1) * (planes // 2), unroll=2)
            def _(z):
                out[k, z] += returned[k, z]

        store(k).start()

    for k in range(members):
        store(k).wait()
    for k in range(members):
        for part in range(2):
            back_copy(k, part).wait_send()

    @pl.loop(0, pairs)
    def _(p):
        face_copy(p).wait_send()
        edge_copy(p).wait_send()

    @pl.when(jnp.logical_not(last))
    def _():
        @pl.loop(0, pairs)
        def _(p):
            down_copy(p).wait_send()

    @pl.when(jnp.logical_not(first))
    def _():
        @pl.loop(0, pairs)
        def _(p):
            up_copy(p).wait_send()


def local(bands, slabs, orbitals, occupation, assignment, pair_live):
    members, planes, points, _ = orbitals.shape
    pairs = members * members
    right, left, diagonal = tables(points)
    vmem = pl.BlockSpec(memory_space=pltpu.VMEM)
    smem = pl.BlockSpec(memory_space=pltpu.SMEM)
    block = pltpu.VMEM((members, planes, points, points), jnp.float32)
    half = pltpu.VMEM((pairs, points // 2, points), jnp.float32)
    twice = pltpu.VMEM((pairs, 2, points // 2, points), jnp.float32)
    quad = pltpu.VMEM((pairs, 2, 2, points // 2, points), jnp.float32)
    column = pltpu.VMEM((planes, points, points), jnp.float32)
    dma = pltpu.SemaphoreType.DMA
    return pl.pallas_call(
        functools.partial(kernel, bands, slabs),
        out_shape=jax.ShapeDtypeStruct(orbitals.shape, jnp.float32),
        in_specs=[pl.BlockSpec(memory_space=pl.ANY), smem, smem, smem, vmem, vmem, vmem],
        out_specs=pl.BlockSpec(memory_space=pl.ANY),
        scratch_shapes=[
            block, block, block, block, block,
            pltpu.VMEM((pairs, planes, points, points), jnp.float32),
            half, half, half, half,
            quad, twice, quad, twice, twice,
            column, column,
            pltpu.VMEM((11, points // 2, points), jnp.float32),
            pltpu.VMEM((2, points, points), jnp.float32),
            pltpu.VMEM((members, 8, points), jnp.float32),
            pltpu.VMEM((members, 8, points), jnp.float32),
            dma((members,)), dma((members,)), dma, dma, dma((members, 2)), dma((members, 2)),
            *[dma((pairs,)) for _ in range(8)],
            dma, dma((members,)),
        ],
        compiler_params=pltpu.CompilerParams(
            collective_id=0, has_side_effects=True, vmem_limit_bytes=60000 * 1024
        ),
    )(
        orbitals, occupation, assignment, pair_live,
        jnp.asarray(right), jnp.asarray(left), jnp.asarray(diagonal),
    )


def solution(mesh):
    placed = (P("band", "slab", None, None), P(), P("band"), P("band", None))
    return jax.shard_map(
        functools.partial(local, mesh.shape["band"], mesh.shape["slab"]),
        mesh=mesh, in_specs=placed, out_specs=P("band", "slab", None, None), check_vma=False,
    )
```
